32 devices in a mesh: team: 8 (over z, core), member: 4 (over y, x).
Axes of the slice: x: 2, y: 2, z: 4, core: 2. Of those that a mesh axis runs over, the one named last changes fastest.
Arguments:
- state_start: float32 [24, 512, 512], P(None, 'team', 'member'), may hold values from -6 to 6
- state_section: float32 [24, 512, 512], P(None, 'team', 'member'), may hold values from -6 to 6
- velocity: float32 [2, 512, 512], P(None, 'team', 'member'), may hold values from -3 to 3
- diffusivity: float32 [24], replicated, may hold values from 0.05 to 0.5
- flame_cells: int32 [32, 128], P(('team', 'member')), may hold values from 0 to 8191, as said below
- block_team: int32 [32, 1], replicated, may hold values from 0 to 7; in each aligned block of 4 rows (0 to 3, 4 to 7, ...) at most 2 rows name the same one
- w_in: bfloat16 [8, 4, 1600, 24], P('team', 'member'), may hold values from -1.25 to 1.25
- w_mid: bfloat16 [8, 4, 800, 1600], P('team', 'member'), may hold values from -0.15625 to 0.15625
- w_low: bfloat16 [8, 4, 400, 800], P('team', 'member'), may hold values from -0.21875 to 0.21875
- w_out: bfloat16 [8, 4, 24, 400], P('team', 'member'), may hold values from -0.3125 to 0.3125
Outputs:
- source_rates: float32 [24, 512, 512], P(None, 'team', 'member')
- new_state: float32 [24, 512, 512], P(None, 'team', 'member')
The draws below stay inside these ranges and needn't reach their ends.
Inputs may be any that keep to these rules, and one draw needn't show every extreme that they name: `flame_cells`: the 128 entries of the rows of one device (rows d * 1 to d + 1 - 1) are distinct cells of that device's tile, given as i * 128 + j. `block_team`: in each aligned block of 4 rows (the flame blocks of one index of team) no regime appears more than 2 times.
All inputs are finite; a program needn't handle non-finite values.
Results may differ from the reference program's by a relative error of at most 0.0017.
The reference program's roundings to bfloat16 on the way (of `inputs`, `hidden_one`, `hidden_two` and `hidden_three`) count: a program that leaves them out, or rounds other values in their place, can miss the bound.
Values may be sent and summed in bfloat16 or wider, within the bound.
A program may use at most 64 MiB of HBM per device.

```python
import math
import jax
import jax.numpy as jnp
import numpy as np
from jax import lax

F = 24
H1 = 1600
H2 = 800
H3 = 400
BLOCK = 128
BLK_DEV = 1
CAP = 2
CX = 64
CY = 128
NX = 512
NY = 512
REGIMES = 8
NETS = 4
BLOCKS = 32
N_TEAM = 8
N_MEMBER = 4


def draw_flame_cells(key, part):
    owners = N_TEAM * N_MEMBER
    key_list = jax.random.split(jax.random.fold_in(key, 11), owners)

    def pick_cells(subkey):
        shuffled = jax.random.permutation(subkey, CX * CY)
        return shuffled[:BLK_DEV * BLOCK]
    flame_rows = jax.vmap(pick_cells)(key_list)
    return flame_rows.reshape(BLK_DEV * owners, BLOCK).astype(jnp.int32)


def level_of(rng, extent, cuts, low, top_value):
    def one(axis_at, blocks):
        steps = jax.random.uniform(jax.random.fold_in(jax.random.fold_in(rng, 6), axis_at), (blocks,), jnp.float32, low / len(cuts), top_value / len(cuts))
        return jnp.repeat(jnp.exp(steps), extent[axis_at] // blocks).reshape((-1,) + (1,) * (len(extent) - axis_at - 1))

    level = one(*cuts[0])
    for cut in cuts[1:]:
        level = level * one(*cut)
    return level


def shared_out(key, own, number, rows, number_of, top, most, lean):
    ranking = jax.random.permutation(key, number_of)
    packed, ordinary = portions_of(number_of, rows * top, most, lean, True), portions_of(number_of, rows * top, most, lean, False)
    places = jnp.arange(number_of)

    def named(tallies, rotation):
        used = int((tallies > 0).sum())
        fixed = max(1, used // 4)
        moved = fixed + (places - fixed + rotation * (used - fixed)) % max(1, number_of - fixed)
        return jnp.zeros((number_of,), jnp.int32).at[ranking[jnp.where(places < fixed, places, moved)]].set(jnp.asarray(tallies, jnp.int32))

    tallies = jnp.where(number % 4 == 0, named(packed, number // 4), named(ordinary, number - number // 4 - 1))
    mixed = jax.random.permutation(jax.random.fold_in(own, 3), number_of)
    source_of, sink = mixed[0:number_of // 2 * 2:2], mixed[1:number_of // 2 * 2:2]
    margin = jnp.minimum(tallies[source_of] - 1, most - tallies[sink]) // 2
    margin = jnp.where((source_of == ranking[0]) | (sink == ranking[0]) | (tallies[sink] == 0), 0, jnp.maximum(margin, 0))
    moved = jax.random.randint(jax.random.fold_in(own, 4), (number_of // 2,), 0, 1 << 20) % (margin + 1)
    tallies = tallies.at[source_of].add(-moved).at[sink].add(moved)
    items = jnp.searchsorted(jnp.cumsum(tallies), jnp.arange(rows * top), side="right").astype(jnp.int32)
    listing = items.reshape(top, rows).T
    listing = listing[jax.random.permutation(jax.random.fold_in(own, 1), rows)]
    rotation = jax.random.randint(jax.random.fold_in(own, 2), (rows, 1), 0, top)
    return jnp.take_along_axis(listing, (jnp.arange(top)[None, :] + rotation) % top, axis=1)


def portions_of(amount, total, bound, lean, full):
    portions = [(1 << 20) // math.isqrt(standing ** lean) + 1 for standing in range(1, amount + 1)]
    largest = bound if full else min(bound, max(-(-total // amount), total * portions[0] // sum(portions)))
    least = 1 if total - largest >= amount - 1 else 0
    counts, spare = [largest] + [least] * (amount - 1), total - largest - least * (amount - 1)
    while spare > 0:
        candidates = [i for i in range(1, amount) if counts[i] < largest] or [i for i in range(1, amount) if counts[i] < bound]
        pool, remaining = sum([portions[i] for i in candidates]), spare
        for i in candidates:
            extra = min(bound - counts[i], max(1, remaining * portions[i] // pool), spare)
            counts[i] = counts[i] + extra
            spare = spare - extra
    return np.array(counts)


def normal_values(own_key, shape, width, bound, cuts=(), held_as=jnp.bfloat16):
    array = width * jax.random.normal(own_key, shape, jnp.float32)
    if cuts:
        array = array * level_of(own_key, shape, cuts, -0.22, 0.18)
    return jnp.clip(array, -bound, bound).astype(held_as)


def setup_inputs(seed: int = 0) -> dict:
    streams_of = jax.random.split(jax.random.key(seed), 11)
    state_start = normal_values(streams_of[0], (F, NX, NY), 1.0, 6.0, ((1, 8), (2, 4)), jnp.float32)
    state_section = normal_values(streams_of[1], (F, NX, NY), 1.0, 6.0, ((1, 8), (2, 4)), jnp.float32)
    velocity = normal_values(streams_of[2], (2, NX, NY), 0.7, 3.0, ((1, 8), (2, 4)), jnp.float32)
    diffusivity = jnp.clip(jnp.exp(jax.random.uniform(streams_of[3], (F,), jnp.float32, math.log(0.05), math.log(0.5))), 0.05, 0.5)
    flame_cells = draw_flame_cells(jax.random.fold_in(streams_of[10], 71), 0)
    block_team_keys = jax.random.split(jax.random.fold_in(streams_of[5], 1), BLOCKS // (N_MEMBER * BLK_DEV))
    block_team_turns = jax.random.permutation(jax.random.fold_in(streams_of[5], 3), BLOCKS // (N_MEMBER * BLK_DEV))
    block_team = jax.vmap(lambda own, number: shared_out(jax.random.fold_in(streams_of[5], 2), own, number, N_MEMBER * BLK_DEV, N_TEAM, 1, CAP, 2))(block_team_keys, block_team_turns).reshape((BLOCKS, 1))
    w_in = normal_values(streams_of[6], (REGIMES, NETS, H1, F), F ** -0.5, 1.25, ((0, 8), (1, 4)))
    w_mid = normal_values(streams_of[7], (REGIMES, NETS, H2, H1), H1 ** -0.5, 0.15625, ((0, 8), (1, 4)))
    w_low = normal_values(streams_of[8], (REGIMES, NETS, H3, H2), H2 ** -0.5, 0.21875, ((0, 8), (1, 4)))
    w_out = normal_values(streams_of[9], (REGIMES, NETS, F, H3), H3 ** -0.5, 0.3125, ((0, 8), (1, 4)))
    return dict(state_start=state_start, state_section=state_section, velocity=velocity, diffusivity=diffusivity, flame_cells=flame_cells, block_team=block_team, w_in=w_in, w_mid=w_mid, w_low=w_low, w_out=w_out)


TIME_STEP = 0.25


def flow_operator(state_section, velocity, diffusivity):
    plus_x = jnp.roll(state_section, -1, axis=1)
    minus_x = jnp.roll(state_section, 1, axis=1)
    plus_y = jnp.roll(state_section, -1, axis=2)
    minus_y = jnp.roll(state_section, 1, axis=2)
    spread = diffusivity[:, None, None] * (plus_x + minus_x + plus_y + minus_y - 4.0 * state_section)
    advect = 0.5 * velocity[0][None] * (plus_x - minus_x) + 0.5 * velocity[1][None] * (plus_y - minus_y)
    return spread - advect


def network_sum(states, weight_in, weight_mid, weight_low, weight_out):
    highest = lax.Precision.HIGHEST
    layer_one = jnp.einsum("nhf,fk->nhk", weight_in.astype(jnp.float32), states.astype(jnp.float32), precision=highest)
    hidden_one = jax.nn.silu(layer_one).astype(jnp.bfloat16)
    layer_two = jnp.einsum("nih,nhk->nik", weight_mid.astype(jnp.float32), hidden_one.astype(jnp.float32), precision=highest)
    hidden_two = jax.nn.silu(layer_two).astype(jnp.bfloat16)
    layer_three = jnp.einsum("nji,nik->njk", weight_low.astype(jnp.float32), hidden_two.astype(jnp.float32), precision=highest)
    hidden_three = jax.nn.silu(layer_three).astype(jnp.bfloat16)
    return jnp.einsum("nfj,njk->fk", weight_out.astype(jnp.float32), hidden_three.astype(jnp.float32), precision=highest)


def reference(state_start, state_section, velocity, diffusivity, flame_cells, block_team, w_in, w_mid, w_low, w_out):
    block_ids = jnp.arange(BLOCKS, dtype=jnp.int32)
    owners = block_ids // BLK_DEV
    grid_x = ((owners // N_MEMBER)[:, None] * CX + flame_cells // CY).astype(jnp.int32)
    grid_y = ((owners % N_MEMBER)[:, None] * CY + flame_cells % CY).astype(jnp.int32)
    gathered = jnp.transpose(state_section[:, grid_x, grid_y], (1, 0, 2)).astype(jnp.bfloat16)

    def block_rates(inputs):
        states, regime = inputs
        return network_sum(states, w_in[regime], w_mid[regime], w_low[regime], w_out[regime])

    block_values = lax.map(block_rates, (gathered, block_team[:, 0]))
    source_rates = jnp.zeros(state_section.shape, jnp.float32).at[:, grid_x, grid_y].add(jnp.transpose(block_values, (1, 0, 2)))
    flow = flow_operator(state_section, velocity, diffusivity)
    new_state = 0.75 * state_start + 0.25 * (state_section + TIME_STEP * (flow + source_rates))
    return source_rates, new_state
```

```python
import functools

import jax
import jax.numpy as jnp
from jax import lax
from jax.experimental import pallas as pl
from jax.experimental.pallas import tpu as pltpu
from jax.sharding import PartitionSpec as P

CAP = 2
TIME_STEP = 0.25
MESH = pl.DeviceIdType.MESH
VMEM = pltpu.VMEM
F32 = jnp.float32
BF16 = jnp.bfloat16


def spread_order(count):
    order = []
    for step in range(1, count // 2 + 1):
        order.append(step)
        if count - step != step:
            order.append(count - step)
    return order


def split_cells(cells, rows_y):
    shift = rows_y.bit_length() - 1
    assert rows_y == 1 << shift
    return cells >> shift, cells & (rows_y - 1)


def row_mask(cells_x, rows_x):
    count = cells_x.shape[1]
    return lax.broadcasted_iota(jnp.int32, (rows_x, count), 0) == cells_x


def silu(x):
    half = 0.5 * x
    return half + half * jnp.tanh(half)


def greet(team, member, teams, members):
    barrier = pltpu.get_barrier_semaphore()
    for d in range(1, teams):
        pl.semaphore_signal(
            barrier, inc=1, device_id=(lax.rem(team + d, teams), member), device_id_type=MESH
        )
    for e in range(1, members):
        pl.semaphore_signal(
            barrier, inc=1, device_id=(team, lax.rem(member + e, members)), device_id_type=MESH
        )
    return barrier


def share_kernel(
    teams,
    members,
    section_ref,
    cells_ref,
    blocks_ref,
    halo_x_ref,
    halo_y_ref,
    edge_x,
    edge_y,
    send_t,
    recv_t,
    send_m,
    recv_m,
    send_h,
    recv_h,
):
    team = lax.axis_index("team")
    member = lax.axis_index("member")
    barrier = greet(team, member, teams, members)
    fields, rows_x, rows_y = section_ref.shape
    cells_x, cells_y = split_cells(cells_ref[...], rows_y)
    count = cells_x.shape[1]
    pick_y = (lax.broadcasted_iota(jnp.int32, (rows_y, count), 0) == cells_y).astype(F32)
    pick_x = row_mask(cells_x, rows_x)
    flat = section_ref[...].reshape(fields * rows_x, rows_y).astype(BF16)
    taken = jnp.dot(flat, pick_y.astype(BF16), preferred_element_type=F32)
    taken = taken.reshape(fields, rows_x, count)
    own = jnp.sum(jnp.where(pick_x[None], taken, 0.0), axis=1)
    blocks_ref[member, team] = own.astype(BF16)
    edge_x[0] = section_ref[:, rows_x - 1, :].astype(BF16)
    edge_x[1] = section_ref[:, 0, :].astype(BF16)
    lanes = lax.broadcasted_iota(jnp.int32, (rows_x, rows_y), 1)
    low = jnp.zeros((rows_x, rows_y), F32)
    high = jnp.zeros((rows_x, rows_y), F32)
    for f in range(fields):
        plane = section_ref[f]
        here = lanes == f
        high = jnp.where(here, pltpu.roll(plane, (f + 1) % rows_y, 1), high)
        low = jnp.where(here, pltpu.roll(plane, f, 1) if f else plane, low)
    edge_y[0] = high.astype(BF16)
    edge_y[1] = low.astype(BF16)
    pl.semaphore_wait(barrier, teams + members - 2)

    started = []
    t_copies = {}
    for d in spread_order(teams):
        copy = pltpu.make_async_remote_copy(
            src_ref=blocks_ref.at[member, team],
            dst_ref=blocks_ref.at[member, team],
            send_sem=send_t.at[d],
            recv_sem=recv_t.at[d],
            device_id=(lax.rem(team + d, teams), member),
            device_id_type=MESH,
        )
        copy.start()
        t_copies[d] = copy

    def forward(d):
        source = lax.rem(team - d + teams, teams)
        for e in range(1, members):
            copy = pltpu.make_async_remote_copy(
                src_ref=blocks_ref.at[member, source],
                dst_ref=blocks_ref.at[member, source],
                send_sem=send_m.at[d, e],
                recv_sem=recv_m.at[d, e],
                device_id=(team, lax.rem(member + e, members)),
                device_id_type=MESH,
            )
            copy.start()
            started.append(copy)

    forward(0)
    halos = []
    for k, (step, edge, halo, along) in enumerate(
        (
            (1, edge_x.at[0], halo_x_ref.at[0], "team"),
            (-1, edge_x.at[1], halo_x_ref.at[1], "team"),
            (1, edge_y.at[0], halo_y_ref.at[0], "member"),
            (-1, edge_y.at[1], halo_y_ref.at[1], "member"),
        )
    ):
        if along == "team":
            device = (lax.rem(team + step + teams, teams), member)
        else:
            device = (team, lax.rem(member + step + members, members))
        copy = pltpu.make_async_remote_copy(
            src_ref=edge,
            dst_ref=halo,
            send_sem=send_h.at[k],
            recv_sem=recv_h.at[k],
            device_id=device,
            device_id_type=MESH,
        )
        copy.start()
        halos.append(copy)
    for d in spread_order(teams):
        t_copies[d].wait_recv()
        forward(d)
    for copy in started + halos:
        copy.wait()
    for d in spread_order(teams):
        t_copies[d].wait_send()


def network_kernel(
    teams,
    members,
    team_of,
    blocks_ref,
    w_in,
    w_mid,
    w_low,
    w_out,
    slots_ref,
    first_weight,
    hidden_one,
    hidden_two,
    hidden_three,
    pick,
    place,
):
    team = lax.axis_index("team")
    fields, count = slots_ref.shape[1:]
    slots_ref[...] = jnp.zeros_like(slots_ref)

    def scan_team(p, found):
        seen = jnp.int32(0)
        for q in range(members):
            mine = (team_of[p * members + q] == team).astype(jnp.int32)
            pick[found] = q * teams + p
            place[found] = p * CAP + seen
            found = found + mine
            seen = seen + mine
        return found

    first_weight[0, 0] = w_in[0, 0].T
    found = lax.fori_loop(0, teams, scan_team, jnp.int32(0))
    last = jnp.maximum(found - 1, 0)
    pick[found] = pick[last]
    place[found] = place[last]

    def layer(weight, source, target, rows):
        total = weight.shape[2]
        start = 0
        while start < total:
            size = min(rows, total - start)
            span = pl.ds(start, size)
            out = jnp.dot(weight[0, 0, span, :], source, preferred_element_type=F32)
            target[span, :] = silu(out).astype(BF16)
            start += size

    def chunk(i, carry):
        first, second = 2 * i, 2 * i + 1
        states = jnp.concatenate([blocks_ref[pick[first]], blocks_ref[pick[second]]], axis=1)
        layer(first_weight, states, hidden_one, 320)
        layer(w_mid, hidden_one[...], hidden_two, 160)
        layer(w_low, hidden_two[...], hidden_three, 80)
        rates = jnp.dot(w_out[0, 0], hidden_three[...], preferred_element_type=F32)
        slots_ref[place[first]] = rates[:, :count]
        slots_ref[place[second]] = rates[:, count:]
        return carry

    lax.fori_loop(0, (found + 1) // 2, chunk, 0)


def return_kernel(
    teams,
    members,
    team_of,
    slots_ref,
    own_ref,
    back,
    chosen,
    got,
    send_t,
    recv_t,
    send_m,
    recv_m,
):
    team = lax.axis_index("team")
    member = lax.axis_index("member")
    barrier = greet(team, member, teams, members)
    pl.semaphore_wait(barrier, teams + members - 2)
    copies = []
    for d in spread_order(teams):
        target = lax.rem(team + d, teams)
        copy = pltpu.make_async_remote_copy(
            src_ref=slots_ref.at[pl.ds(target * CAP, CAP)],
            dst_ref=back.at[pl.ds(team * CAP, CAP)],
            send_sem=send_t.at[d],
            recv_sem=recv_t.at[d],
            device_id=(target, member),
            device_id_type=MESH,
        )
        copy.start()
        copies.append(copy)
    back[pl.ds(team * CAP, CAP)] = slots_ref[pl.ds(team * CAP, CAP)]
    assigned = [team_of[team * members + q] for q in range(members)]
    where = []
    for q in range(members):
        rank = jnp.int32(0)
        for other in range(q):
            rank = rank + (assigned[other] == assigned[q]).astype(jnp.int32)
        where.append(assigned[q] * CAP + rank)
    for copy in copies:
        copy.wait_recv()
    for q in range(members):
        chosen[q] = back[where[q]]
    sends = []
    for e in range(1, members):
        target = lax.rem(member + e, members)
        copy = pltpu.make_async_remote_copy(
            src_ref=chosen.at[target],
            dst_ref=got.at[e],
            send_sem=send_m.at[e],
            recv_sem=recv_m.at[e],
            device_id=(team, target),
            device_id_type=MESH,
        )
        copy.start()
        sends.append(copy)
    total = chosen[member]
    for e, copy in enumerate(sends):
        copy.wait_recv()
        total = total + got[e + 1]
    own_ref[...] = total
    for copy in copies + sends:
        copy.wait_send()


def update_kernel(
    start_ref,
    section_ref,
    velocity_ref,
    spread_ref,
    cells_ref,
    rates_ref,
    halo_x_ref,
    halo_y_ref,
    source_ref,
    new_ref,
):
    fields, rows_x, rows_y = section_ref.shape
    step = pl.program_id(0)
    cells_x, cells_y = split_cells(cells_ref[...], rows_y)
    count = cells_x.shape[1]
    pick_x = row_mask(cells_x, rows_x)
    pick_y = (lax.broadcasted_iota(jnp.int32, (rows_y, count), 0) == cells_y).astype(F32)
    pick_y = pick_y.astype(BF16)
    pick_y = jnp.concatenate([pick_y, pick_y], axis=1)
    lanes = lax.broadcasted_iota(jnp.int32, (rows_x, rows_y), 1)
    subs = lax.broadcasted_iota(jnp.int32, (rows_x, rows_y), 0)
    low_y = halo_y_ref[0].astype(F32)
    high_y = halo_y_ref[1].astype(F32)
    half_u = 0.5 * velocity_ref[0]
    half_v = 0.5 * velocity_ref[1]
    for f in range(fields):
        spread_rates = jnp.where(pick_x, rates_ref[f : f + 1, :], 0.0)
        top = spread_rates.astype(BF16)
        rest = (spread_rates - top.astype(F32)).astype(BF16)
        source = lax.dot_general(
            jnp.concatenate([top, rest], axis=1),
            pick_y,
            (((1,), (1,)), ((), ())),
            preferred_element_type=F32,
        )
        here = section_ref[f]
        field = step * fields + f
        plus_x = jnp.where(
            subs == rows_x - 1,
            halo_x_ref[1, f : f + 1, :],
            pltpu.roll(here, rows_x - 1, 0),
        )
        minus_x = jnp.where(
            subs == 0, halo_x_ref[0, f : f + 1, :], pltpu.roll(here, 1, 0)
        )
        plus_y = jnp.where(
            lanes == rows_y - 1,
            pltpu.roll(high_y, rows_y - 1 - field, 1),
            pltpu.roll(here, rows_y - 1, 1),
        )
        minus_y = jnp.where(
            lanes == 0, pltpu.roll(low_y, lax.rem(rows_y - field, rows_y), 1), pltpu.roll(here, 1, 1)
        )
        flow = (
            spread_ref[field] * (plus_x + minus_x + plus_y + minus_y - 4.0 * here)
            - half_u * (plus_x - minus_x)
            - half_v * (plus_y - minus_y)
        )
        source_ref[f] = source
        new_ref[f] = 0.75 * start_ref[f] + 0.25 * (here + TIME_STEP * (flow + source))


def whole(space=VMEM):
    return pl.BlockSpec(memory_space=space)


def shards(
    state_start,
    state_section,
    velocity,
    diffusivity,
    flame_cells,
    block_team,
    w_in,
    w_mid,
    w_low,
    w_out,
):
    teams = lax.axis_size("team")
    members = lax.axis_size("member")
    fields, rows_x, rows_y = state_section.shape
    count = flame_cells.shape[1]
    team_of = block_team.reshape(-1)
    dma = pltpu.SemaphoreType.DMA
    blocks, halo_x, halo_y = pl.pallas_call(
        functools.partial(share_kernel, teams, members),
        out_shape=(
            jax.ShapeDtypeStruct((members, teams, fields, count), BF16),
            jax.ShapeDtypeStruct((2, fields, rows_y), BF16),
            jax.ShapeDtypeStruct((2, rows_x, rows_y), BF16),
        ),
        in_specs=[whole(), whole()],
        out_specs=(whole(), whole(), whole()),
        scratch_shapes=[
            VMEM((2, fields, rows_y), BF16),
            VMEM((2, rows_x, rows_y), BF16),
            dma((teams,)),
            dma((teams,)),
            dma((teams, members)),
            dma((teams, members)),
            dma((4,)),
            dma((4,)),
        ],
        compiler_params=pltpu.CompilerParams(collective_id=0, has_side_effects=True),
        name="share",
    )(state_section, flame_cells)
    slots = pl.pallas_call(
        functools.partial(network_kernel, teams, members),
        out_shape=jax.ShapeDtypeStruct((teams * CAP, fields, count), F32),
        in_specs=[whole(pltpu.SMEM)] + [whole()] * 5,
        out_specs=whole(),
        scratch_shapes=[
            VMEM(w_in.shape, BF16),
            VMEM((w_in.shape[2], 2 * count), BF16),
            VMEM((w_mid.shape[2], 2 * count), BF16),
            VMEM((w_low.shape[2], 2 * count), BF16),
            pltpu.SMEM((teams * CAP + 2,), jnp.int32),
            pltpu.SMEM((teams * CAP + 2,), jnp.int32),
        ],
        name="networks",
    )(team_of, blocks.reshape(members * teams, fields, count), jnp.swapaxes(w_in, 2, 3), w_mid, w_low, w_out)
    rates = pl.pallas_call(
        functools.partial(return_kernel, teams, members),
        out_shape=jax.ShapeDtypeStruct((fields, count), F32),
        in_specs=[whole(pltpu.SMEM), whole()],
        out_specs=whole(),
        scratch_shapes=[
            VMEM((teams * CAP, fields, count), F32),
            VMEM((members, fields, count), F32),
            VMEM((members, fields, count), F32),
            dma((teams,)),
            dma((teams,)),
            dma((members,)),
            dma((members,)),
        ],
        compiler_params=pltpu.CompilerParams(collective_id=1, has_side_effects=True),
        name="giveback",
    )(team_of, slots)
    step = 8 if fields % 8 == 0 else fields
    tile = pl.BlockSpec((step, rows_x, rows_y), lambda i: (i, 0, 0))
    return pl.pallas_call(
        update_kernel,
        grid=(fields // step,),
        out_shape=(
            jax.ShapeDtypeStruct(state_section.shape, F32),
            jax.ShapeDtypeStruct(state_section.shape, F32),
        ),
        in_specs=[
            tile,
            tile,
            pl.BlockSpec(velocity.shape, lambda i: (0, 0, 0)),
            pl.BlockSpec(memory_space=pltpu.SMEM),
            pl.BlockSpec(flame_cells.shape, lambda i: (0, 0)),
            pl.BlockSpec((step, count), lambda i: (i, 0)),
            pl.BlockSpec((2, step, rows_y), lambda i: (0, i, 0)),
            pl.BlockSpec(halo_y.shape, lambda i: (0, 0, 0)),
        ],
        out_specs=(tile, tile),
        name="update",
    )(
        state_start,
        state_section,
        velocity,
        diffusivity,
        flame_cells,
        rates,
        halo_x.astype(F32),
        halo_y,
    )


def solution(mesh):
    grid = P(None, "team", "member")
    weights = P("team", "member", None, None)
    placed = (
        grid,
        grid,
        grid,
        P(),
        P(("team", "member"), None),
        P(),
        weights,
        weights,
        weights,
        weights,
    )
    return jax.shard_map(
        shards, mesh=mesh, in_specs=placed, out_specs=(grid, grid), check_vma=False
    )
```

```python
import functools

import jax
import jax.numpy as jnp
from jax import lax
from jax.experimental import pallas as pl
from jax.experimental.pallas import tpu as pltpu
from jax.sharding import PartitionSpec as P

CAP = 2
TIME_STEP = 0.25
GRANT = 16 << 20
MESH = pl.DeviceIdType.MESH
VMEM = pltpu.VMEM
F32 = jnp.float32
BF16 = jnp.bfloat16


def spread_order(count):
    order = []
    for step in range(1, count // 2 + 1):
        order.append(step)
        if count - step != step:
            order.append(count - step)
    return order


def split_cells(cells, rows_y):
    shift = rows_y.bit_length() - 1
    assert rows_y == 1 << shift
    return cells >> shift, cells & (rows_y - 1)


def row_mask(cells_x, rows_x):
    count = cells_x.shape[1]
    return lax.broadcasted_iota(jnp.int32, (rows_x, count), 0) == cells_x


def silu(x):
    half = 0.5 * x
    return half + half * jnp.tanh(half)


def greet(team, member, teams, members):
    barrier = pltpu.get_barrier_semaphore()
    for d in range(1, teams):
        pl.semaphore_signal(
            barrier, inc=1, device_id=(lax.rem(team + d, teams), member), device_id_type=MESH
        )
    for e in range(1, members):
        pl.semaphore_signal(
            barrier, inc=1, device_id=(team, lax.rem(member + e, members)), device_id_type=MESH
        )
    return barrier


def share_kernel(
    teams,
    members,
    section_ref,
    cells_ref,
    blocks_ref,
    halo_x_ref,
    halo_y_ref,
    edge_x,
    edge_y,
    send_t,
    recv_t,
    send_m,
    recv_m,
    send_h,
    recv_h,
):
    team = lax.axis_index("team")
    member = lax.axis_index("member")
    barrier = greet(team, member, teams, members)
    fields, rows_x, rows_y = section_ref.shape
    cells_x, cells_y = split_cells(cells_ref[...], rows_y)
    count = cells_x.shape[1]
    pick_y = (lax.broadcasted_iota(jnp.int32, (rows_y, count), 0) == cells_y).astype(F32)
    pick_x = row_mask(cells_x, rows_x)
    flat = section_ref[...].reshape(fields * rows_x, rows_y).astype(BF16)
    taken = jnp.dot(flat, pick_y.astype(BF16), preferred_element_type=F32)
    taken = taken.reshape(fields, rows_x, count)
    own = jnp.sum(jnp.where(pick_x[None], taken, 0.0), axis=1)
    blocks_ref[member, team] = own.astype(BF16)
    edge_x[0] = section_ref[:, rows_x - 1, :].astype(BF16)
    edge_x[1] = section_ref[:, 0, :].astype(BF16)
    lanes = lax.broadcasted_iota(jnp.int32, (rows_x, rows_y), 1)
    low = jnp.zeros((rows_x, rows_y), F32)
    high = jnp.zeros((rows_x, rows_y), F32)
    for f in range(fields):
        plane = section_ref[f]
        here = lanes == f
        high = jnp.where(here, pltpu.roll(plane, (f + 1) % rows_y, 1), high)
        low = jnp.where(here, pltpu.roll(plane, f, 1) if f else plane, low)
    edge_y[0] = high.astype(BF16)
    edge_y[1] = low.astype(BF16)
    pl.semaphore_wait(barrier, teams + members - 2)

    started = []
    t_copies = {}
    for d in spread_order(teams):
        copy = pltpu.make_async_remote_copy(
            src_ref=blocks_ref.at[member, team],
            dst_ref=blocks_ref.at[member, team],
            send_sem=send_t.at[d],
            recv_sem=recv_t.at[d],
            device_id=(lax.rem(team + d, teams), member),
            device_id_type=MESH,
        )
        copy.start()
        t_copies[d] = copy

    def forward(d):
        source = lax.rem(team - d + teams, teams)
        for e in range(1, members):
            copy = pltpu.make_async_remote_copy(
                src_ref=blocks_ref.at[member, source],
                dst_ref=blocks_ref.at[member, source],
                send_sem=send_m.at[d, e],
                recv_sem=recv_m.at[d, e],
                device_id=(team, lax.rem(member + e, members)),
                device_id_type=MESH,
            )
            copy.start()
            started.append(copy)

    forward(0)
    halos = []
    for k, (step, edge, halo, along) in enumerate(
        (
            (1, edge_x.at[0], halo_x_ref.at[0], "team"),
            (-1, edge_x.at[1], halo_x_ref.at[1], "team"),
            (1, edge_y.at[0], halo_y_ref.at[0], "member"),
            (-1, edge_y.at[1], halo_y_ref.at[1], "member"),
        )
    ):
        if along == "team":
            device = (lax.rem(team + step + teams, teams), member)
        else:
            device = (team, lax.rem(member + step + members, members))
        copy = pltpu.make_async_remote_copy(
            src_ref=edge,
            dst_ref=halo,
            send_sem=send_h.at[k],
            recv_sem=recv_h.at[k],
            device_id=device,
            device_id_type=MESH,
        )
        copy.start()
        halos.append(copy)
    for d in spread_order(teams):
        t_copies[d].wait_recv()
        forward(d)
    for copy in started + halos:
        copy.wait()
    for d in spread_order(teams):
        t_copies[d].wait_send()


def network_kernel(
    teams,
    members,
    team_of,
    blocks_ref,
    w_in,
    w_mid,
    w_low,
    w_out,
    slots_ref,
    first_weight,
    hidden_one,
    hidden_two,
    hidden_three,
    pick,
    place,
):
    team = lax.axis_index("team")
    fields, count = slots_ref.shape[1:]
    slots_ref[...] = jnp.zeros_like(slots_ref)

    def scan_team(p, found):
        seen = jnp.int32(0)
        for q in range(members):
            mine = (team_of[p * members + q] == team).astype(jnp.int32)
            pick[found] = q * teams + p
            place[found] = p * CAP + seen
            found = found + mine
            seen = seen + mine
        return found

    first_weight[0, 0] = w_in[0, 0].T
    found = lax.fori_loop(0, teams, scan_team, jnp.int32(0))
    last = jnp.maximum(found - 1, 0)
    pick[found] = pick[last]
    place[found] = place[last]

    def layer(weight, source, target, rows):
        total = weight.shape[2]
        start = 0
        while start < total:
            size = min(rows, total - start)
            span = pl.ds(start, size)
            out = jnp.dot(weight[0, 0, span, :], source, preferred_element_type=F32)
            target[span, :] = silu(out).astype(BF16)
            start += size

    def chunk(i, carry):
        first, second = 2 * i, 2 * i + 1
        states = jnp.concatenate([blocks_ref[pick[first]], blocks_ref[pick[second]]], axis=1)
        layer(first_weight, states, hidden_one, 320)
        layer(w_mid, hidden_one[...], hidden_two, 160)
        layer(w_low, hidden_two[...], hidden_three, 80)
        rates = jnp.dot(w_out[0, 0], hidden_three[...], preferred_element_type=F32)
        slots_ref[place[first]] = rates[:, :count]
        slots_ref[place[second]] = rates[:, count:]
        return carry

    lax.fori_loop(0, (found + 1) // 2, chunk, 0)


def flow_base(
    start_ref, section_ref, velocity_ref, spread_ref, halo_x_ref, halo_y_ref, base_ref
):
    fields, rows_x, rows_y = section_ref.shape
    lanes = lax.broadcasted_iota(jnp.int32, (rows_x, rows_y), 1)
    subs = lax.broadcasted_iota(jnp.int32, (rows_x, rows_y), 0)
    half_u = 0.5 * velocity_ref[0]
    half_v = 0.5 * velocity_ref[1]
    low_x = halo_x_ref[0].astype(F32)
    high_x = halo_x_ref[1].astype(F32)
    low_y = halo_y_ref[0].astype(F32)
    high_y = halo_y_ref[1].astype(F32)
    for f in range(fields):
        here = section_ref[f]
        plus_x = jnp.where(
            subs == rows_x - 1, high_x[f : f + 1], pltpu.roll(here, rows_x - 1, 0)
        )
        minus_x = jnp.where(subs == 0, low_x[f : f + 1], pltpu.roll(here, 1, 0))
        plus_y = jnp.where(
            lanes == rows_y - 1,
            pltpu.roll(high_y, rows_y - 1 - f, 1),
            pltpu.roll(here, rows_y - 1, 1),
        )
        edge = pltpu.roll(low_y, (rows_y - f) % rows_y, 1) if f else low_y
        minus_y = jnp.where(lanes == 0, edge, pltpu.roll(here, 1, 1))
        flow = (
            spread_ref[f] * (plus_x + minus_x + plus_y + minus_y - 4.0 * here)
            - half_u * (plus_x - minus_x)
            - half_v * (plus_y - minus_y)
        )
        base_ref[f] = 0.75 * start_ref[f] + 0.25 * (here + TIME_STEP * flow)


def return_kernel(
    teams,
    members,
    team_of,
    spread_ref,
    slots_ref,
    start_ref,
    section_ref,
    velocity_ref,
    halo_x_ref,
    halo_y_ref,
    own_ref,
    base_ref,
    back,
    chosen,
    got,
    send_t,
    recv_t,
    send_m,
    recv_m,
):
    team = lax.axis_index("team")
    member = lax.axis_index("member")
    barrier = greet(team, member, teams, members)
    pl.semaphore_wait(barrier, teams + members - 2)
    copies = []
    for d in spread_order(teams):
        target = lax.rem(team + d, teams)
        copy = pltpu.make_async_remote_copy(
            src_ref=slots_ref.at[pl.ds(target * CAP, CAP)],
            dst_ref=back.at[pl.ds(team * CAP, CAP)],
            send_sem=send_t.at[d],
            recv_sem=recv_t.at[d],
            device_id=(target, member),
            device_id_type=MESH,
        )
        copy.start()
        copies.append(copy)
    back[pl.ds(team * CAP, CAP)] = slots_ref[pl.ds(team * CAP, CAP)]
    assigned = [team_of[team * members + q] for q in range(members)]
    where = []
    for q in range(members):
        rank = jnp.int32(0)
        for other in range(q):
            rank = rank + (assigned[other] == assigned[q]).astype(jnp.int32)
        where.append(assigned[q] * CAP + rank)
    flow_base(
        start_ref, section_ref, velocity_ref, spread_ref, halo_x_ref, halo_y_ref, base_ref
    )
    for copy in copies:
        copy.wait_recv()
    for q in range(members):
        chosen[q] = back[where[q]]
    sends = []
    for e in range(1, members):
        target = lax.rem(member + e, members)
        copy = pltpu.make_async_remote_copy(
            src_ref=chosen.at[target],
            dst_ref=got.at[e],
            send_sem=send_m.at[e],
            recv_sem=recv_m.at[e],
            device_id=(team, target),
            device_id_type=MESH,
        )
        copy.start()
        sends.append(copy)
    total = chosen[member]
    for e, copy in enumerate(sends):
        copy.wait_recv()
        total = total + got[e + 1]
    own_ref[...] = total
    for copy in copies + sends:
        copy.wait_send()


def update_kernel(cells_ref, rates_ref, base_ref, source_ref, new_ref):
    fields, rows_x, rows_y = base_ref.shape
    cells_x, cells_y = split_cells(cells_ref[...], rows_y)
    count = cells_x.shape[1]
    pick_x = row_mask(cells_x, rows_x)
    pick_y = (lax.broadcasted_iota(jnp.int32, (rows_y, count), 0) == cells_y).astype(F32)
    pick_y = pick_y.astype(BF16)
    pick_y = jnp.concatenate([pick_y, pick_y], axis=1)
    for f in range(fields):
        spread_rates = jnp.where(pick_x, rates_ref[f : f + 1, :], 0.0)
        top = spread_rates.astype(BF16)
        rest = (spread_rates - top.astype(F32)).astype(BF16)
        source = lax.dot_general(
            jnp.concatenate([top, rest], axis=1),
            pick_y,
            (((1,), (1,)), ((), ())),
            preferred_element_type=F32,
        )
        source_ref[f] = source
        new_ref[f] = base_ref[f] + (0.25 * TIME_STEP) * source


def whole(space=VMEM):
    return pl.BlockSpec(memory_space=space)


def shards(
    state_start,
    state_section,
    velocity,
    diffusivity,
    flame_cells,
    block_team,
    w_in,
    w_mid,
    w_low,
    w_out,
):
    teams = lax.axis_size("team")
    members = lax.axis_size("member")
    fields, rows_x, rows_y = state_section.shape
    count = flame_cells.shape[1]
    team_of = block_team.reshape(-1)
    dma = pltpu.SemaphoreType.DMA
    blocks, halo_x, halo_y = pl.pallas_call(
        functools.partial(share_kernel, teams, members),
        out_shape=(
            jax.ShapeDtypeStruct((members, teams, fields, count), BF16),
            jax.ShapeDtypeStruct((2, fields, rows_y), BF16),
            jax.ShapeDtypeStruct((2, rows_x, rows_y), BF16),
        ),
        in_specs=[whole(), whole()],
        out_specs=(whole(), whole(), whole()),
        scratch_shapes=[
            VMEM((2, fields, rows_y), BF16),
            VMEM((2, rows_x, rows_y), BF16),
            dma((teams,)),
            dma((teams,)),
            dma((teams, members)),
            dma((teams, members)),
            dma((4,)),
            dma((4,)),
        ],
        compiler_params=pltpu.CompilerParams(
            collective_id=0, has_side_effects=True, vmem_limit_bytes=GRANT
        ),
        name="share",
    )(state_section, flame_cells)
    slots = pl.pallas_call(
        functools.partial(network_kernel, teams, members),
        out_shape=jax.ShapeDtypeStruct((teams * CAP, fields, count), F32),
        in_specs=[whole(pltpu.SMEM)] + [whole()] * 5,
        out_specs=whole(),
        scratch_shapes=[
            VMEM(w_in.shape, BF16),
            VMEM((w_in.shape[2], 2 * count), BF16),
            VMEM((w_mid.shape[2], 2 * count), BF16),
            VMEM((w_low.shape[2], 2 * count), BF16),
            pltpu.SMEM((teams * CAP + 2,), jnp.int32),
            pltpu.SMEM((teams * CAP + 2,), jnp.int32),
        ],
        compiler_params=pltpu.CompilerParams(vmem_limit_bytes=GRANT),
        name="networks",
    )(team_of, blocks.reshape(members * teams, fields, count), jnp.swapaxes(w_in, 2, 3), w_mid, w_low, w_out)
    rates, base = pl.pallas_call(
        functools.partial(return_kernel, teams, members),
        out_shape=(
            jax.ShapeDtypeStruct((fields, count), F32),
            jax.ShapeDtypeStruct(state_section.shape, F32),
        ),
        in_specs=[whole(pltpu.SMEM)] * 2 + [whole()] * 6,
        out_specs=(whole(), whole()),
        scratch_shapes=[
            VMEM((teams * CAP, fields, count), F32),
            VMEM((members, fields, count), F32),
            VMEM((members, fields, count), F32),
            dma((teams,)),
            dma((teams,)),
            dma((members,)),
            dma((members,)),
        ],
        compiler_params=pltpu.CompilerParams(
            collective_id=1, has_side_effects=True, vmem_limit_bytes=GRANT
        ),
        name="giveback",
    )(team_of, diffusivity, slots, state_start, state_section, velocity, halo_x, halo_y)
    step = 8 if fields % 8 == 0 else fields
    tile = pl.BlockSpec((step, rows_x, rows_y), lambda i: (i, 0, 0))
    return pl.pallas_call(
        update_kernel,
        grid=(fields // step,),
        out_shape=(
            jax.ShapeDtypeStruct(state_section.shape, F32),
            jax.ShapeDtypeStruct(state_section.shape, F32),
        ),
        in_specs=[
            pl.BlockSpec(flame_cells.shape, lambda i: (0, 0)),
            pl.BlockSpec((step, count), lambda i: (i, 0)),
            tile,
        ],
        out_specs=(tile, tile),
        compiler_params=pltpu.CompilerParams(vmem_limit_bytes=GRANT),
        name="update",
    )(flame_cells, rates, base)


def solution(mesh):
    grid = P(None, "team", "member")
    weights = P("team", "member", None, None)
    placed = (
        grid,
        grid,
        grid,
        P(),
        P(("team", "member"), None),
        P(),
        weights,
        weights,
        weights,
        weights,
    )
    return jax.shard_map(
        shards, mesh=mesh, in_specs=placed, out_specs=(grid, grid), check_vma=False
    )
```

```python
import functools

import jax
import jax.numpy as jnp
from jax import lax
from jax.experimental import pallas as pl
from jax.experimental.pallas import tpu as pltpu
from jax.sharding import PartitionSpec as P

CAP = 2
TIME_STEP = 0.25
GRANT = 16 << 20
MESH = pl.DeviceIdType.MESH
VMEM = pltpu.VMEM
F32 = jnp.float32
BF16 = jnp.bfloat16


def spread_order(count):
    order = []
    for step in range(1, count // 2 + 1):
        order.append(step)
        if count - step != step:
            order.append(count - step)
    return order


def split_cells(cells, rows_y):
    shift = rows_y.bit_length() - 1
    assert rows_y == 1 << shift
    return cells >> shift, cells & (rows_y - 1)


def row_mask(cells_x, rows_x):
    count = cells_x.shape[1]
    return lax.broadcasted_iota(jnp.int32, (rows_x, count), 0) == cells_x


def silu(x):
    half = 0.5 * x
    return half + half * jnp.tanh(half)


def greet(team, member, teams, members):
    barrier = pltpu.get_barrier_semaphore()
    for d in range(1, teams):
        pl.semaphore_signal(
            barrier, inc=1, device_id=(lax.rem(team + d, teams), member), device_id_type=MESH
        )
    for e in range(1, members):
        pl.semaphore_signal(
            barrier, inc=1, device_id=(team, lax.rem(member + e, members)), device_id_type=MESH
        )
    return barrier


def share_kernel(
    teams,
    members,
    section_hbm,
    cells_hbm,
    w_in_hbm,
    w_mid_hbm,
    w_low_hbm,
    w_out_hbm,
    blocks_ref,
    halo_x_ref,
    halo_y_ref,
    w_in_ref,
    w_mid_ref,
    w_low_ref,
    w_out_ref,
    section_ref,
    cells_ref,
    w_in_raw,
    edge_x,
    edge_y,
    load_sem,
    send_t,
    recv_t,
    send_m,
    recv_m,
    send_h,
    recv_h,
):
    team = lax.axis_index("team")
    member = lax.axis_index("member")
    barrier = greet(team, member, teams, members)
    loads = []
    for k, (source, target) in enumerate(
        (
            (section_hbm, section_ref),
            (cells_hbm, cells_ref),
            (w_in_hbm, w_in_raw),
            (w_mid_hbm, w_mid_ref),
            (w_low_hbm, w_low_ref),
            (w_out_hbm, w_out_ref),
        )
    ):
        copy = pltpu.make_async_copy(source, target, load_sem.at[k])
        copy.start()
        loads.append(copy)
    loads[1].wait()
    fields, rows_x, rows_y = section_ref.shape
    cells_x, cells_y = split_cells(cells_ref[...], rows_y)
    count = cells_x.shape[1]
    pick_y = (lax.broadcasted_iota(jnp.int32, (rows_y, count), 0) == cells_y).astype(F32)
    pick_x = row_mask(cells_x, rows_x)
    loads[0].wait()
    flat = section_ref[...].reshape(fields * rows_x, rows_y).astype(BF16)
    taken = jnp.dot(flat, pick_y.astype(BF16), preferred_element_type=F32)
    taken = taken.reshape(fields, rows_x, count)
    own = jnp.sum(jnp.where(pick_x[None], taken, 0.0), axis=1)
    blocks_ref[member, team] = own.astype(BF16)
    pl.semaphore_wait(barrier, teams + members - 2)

    started = []
    t_copies = {}
    for d in spread_order(teams):
        copy = pltpu.make_async_remote_copy(
            src_ref=blocks_ref.at[member, team],
            dst_ref=blocks_ref.at[member, team],
            send_sem=send_t.at[d],
            recv_sem=recv_t.at[d],
            device_id=(lax.rem(team + d, teams), member),
            device_id_type=MESH,
        )
        copy.start()
        t_copies[d] = copy

    def forward(d):
        source = lax.rem(team - d + teams, teams)
        for e in range(1, members):
            copy = pltpu.make_async_remote_copy(
                src_ref=blocks_ref.at[member, source],
                dst_ref=blocks_ref.at[member, source],
                send_sem=send_m.at[d, e],
                recv_sem=recv_m.at[d, e],
                device_id=(team, lax.rem(member + e, members)),
                device_id_type=MESH,
            )
            copy.start()
            started.append(copy)

    forward(0)
    edge_x[0] = section_ref[:, rows_x - 1, :].astype(BF16)
    edge_x[1] = section_ref[:, 0, :].astype(BF16)
    lanes = lax.broadcasted_iota(jnp.int32, (rows_x, rows_y), 1)
    low = jnp.zeros((rows_x, rows_y), F32)
    high = jnp.zeros((rows_x, rows_y), F32)
    for f in range(fields):
        plane = section_ref[f]
        here = lanes == f
        high = jnp.where(here, pltpu.roll(plane, (f + 1) % rows_y, 1), high)
        low = jnp.where(here, pltpu.roll(plane, f, 1) if f else plane, low)
    edge_y[0] = high.astype(BF16)
    edge_y[1] = low.astype(BF16)
    halos = []
    for k, (step, edge, halo, along) in enumerate(
        (
            (1, edge_x.at[0], halo_x_ref.at[0], "team"),
            (-1, edge_x.at[1], halo_x_ref.at[1], "team"),
            (1, edge_y.at[0], halo_y_ref.at[0], "member"),
            (-1, edge_y.at[1], halo_y_ref.at[1], "member"),
        )
    ):
        if along == "team":
            device = (lax.rem(team + step + teams, teams), member)
        else:
            device = (team, lax.rem(member + step + members, members))
        copy = pltpu.make_async_remote_copy(
            src_ref=edge,
            dst_ref=halo,
            send_sem=send_h.at[k],
            recv_sem=recv_h.at[k],
            device_id=device,
            device_id_type=MESH,
        )
        copy.start()
        halos.append(copy)
    loads[2].wait()
    w_in_ref[0, 0] = w_in_raw[0, 0].T
    for d in spread_order(teams):
        t_copies[d].wait_recv()
        forward(d)
    for copy in started + halos + loads[3:]:
        copy.wait()
    for d in spread_order(teams):
        t_copies[d].wait_send()


def network_kernel(
    teams,
    members,
    team_of,
    blocks_ref,
    w_in,
    w_mid,
    w_low,
    w_out,
    slots_ref,
    hidden_one,
    hidden_two,
    hidden_three,
    pick,
    place,
):
    team = lax.axis_index("team")
    fields, count = slots_ref.shape[1:]
    slots_ref[...] = jnp.zeros_like(slots_ref)

    def scan_team(p, found):
        seen = jnp.int32(0)
        for q in range(members):
            mine = (team_of[p * members + q] == team).astype(jnp.int32)
            pick[found] = q * teams + p
            place[found] = p * CAP + seen
            found = found + mine
            seen = seen + mine
        return found

    found = lax.fori_loop(0, teams, scan_team, jnp.int32(0))
    last = jnp.maximum(found - 1, 0)
    pick[found] = pick[last]
    place[found] = place[last]

    def layer(weight, source, target, rows):
        total = weight.shape[2]
        start = 0
        while start < total:
            size = min(rows, total - start)
            span = pl.ds(start, size)
            out = jnp.dot(weight[0, 0, span, :], source, preferred_element_type=F32)
            target[span, :] = silu(out).astype(BF16)
            start += size

    def chunk(i, carry):
        first, second = 2 * i, 2 * i + 1
        states = jnp.concatenate([blocks_ref[pick[first]], blocks_ref[pick[second]]], axis=1)
        layer(w_in, states, hidden_one, 320)
        layer(w_mid, hidden_one[...], hidden_two, 160)
        layer(w_low, hidden_two[...], hidden_three, 80)
        rates = jnp.dot(w_out[0, 0], hidden_three[...], preferred_element_type=F32)
        slots_ref[place[first]] = rates[:, :count]
        slots_ref[place[second]] = rates[:, count:]
        return carry

    lax.fori_loop(0, (found + 1) // 2, chunk, 0)


def flow_base(
    start_ref, section_ref, velocity_ref, spread_ref, halo_x_ref, halo_y_ref, base_ref
):
    fields, rows_x, rows_y = section_ref.shape
    lanes = lax.broadcasted_iota(jnp.int32, (rows_x, rows_y), 1)
    subs = lax.broadcasted_iota(jnp.int32, (rows_x, rows_y), 0)
    half_u = 0.5 * velocity_ref[0]
    half_v = 0.5 * velocity_ref[1]
    low_x = halo_x_ref[0].astype(F32)
    high_x = halo_x_ref[1].astype(F32)
    low_y = halo_y_ref[0].astype(F32)
    high_y = halo_y_ref[1].astype(F32)
    for f in range(fields):
        here = section_ref[f]
        plus_x = jnp.where(
            subs == rows_x - 1, high_x[f : f + 1], pltpu.roll(here, rows_x - 1, 0)
        )
        minus_x = jnp.where(subs == 0, low_x[f : f + 1], pltpu.roll(here, 1, 0))
        plus_y = jnp.where(
            lanes == rows_y - 1,
            pltpu.roll(high_y, rows_y - 1 - f, 1),
            pltpu.roll(here, rows_y - 1, 1),
        )
        edge = pltpu.roll(low_y, (rows_y - f) % rows_y, 1) if f else low_y
        minus_y = jnp.where(lanes == 0, edge, pltpu.roll(here, 1, 1))
        flow = (
            spread_ref[f] * (plus_x + minus_x + plus_y + minus_y - 4.0 * here)
            - half_u * (plus_x - minus_x)
            - half_v * (plus_y - minus_y)
        )
        base_ref[f] = 0.75 * start_ref[f] + 0.25 * (here + TIME_STEP * flow)


def return_kernel(
    teams,
    members,
    team_of,
    spread_ref,
    slots_ref,
    start_ref,
    section_ref,
    velocity_ref,
    halo_x_ref,
    halo_y_ref,
    own_ref,
    base_ref,
    back,
    chosen,
    got,
    send_t,
    recv_t,
    send_m,
    recv_m,
):
    team = lax.axis_index("team")
    member = lax.axis_index("member")
    barrier = greet(team, member, teams, members)
    pl.semaphore_wait(barrier, teams + members - 2)
    copies = []
    for d in spread_order(teams):
        target = lax.rem(team + d, teams)
        copy = pltpu.make_async_remote_copy(
            src_ref=slots_ref.at[pl.ds(target * CAP, CAP)],
            dst_ref=back.at[pl.ds(team * CAP, CAP)],
            send_sem=send_t.at[d],
            recv_sem=recv_t.at[d],
            device_id=(target, member),
            device_id_type=MESH,
        )
        copy.start()
        copies.append(copy)
    back[pl.ds(team * CAP, CAP)] = slots_ref[pl.ds(team * CAP, CAP)]
    assigned = [team_of[team * members + q] for q in range(members)]
    where = []
    for q in range(members):
        rank = jnp.int32(0)
        for other in range(q):
            rank = rank + (assigned[other] == assigned[q]).astype(jnp.int32)
        where.append(assigned[q] * CAP + rank)
    flow_base(
        start_ref, section_ref, velocity_ref, spread_ref, halo_x_ref, halo_y_ref, base_ref
    )
    for copy in copies:
        copy.wait_recv()
    for q in range(members):
        chosen[q] = back[where[q]]
    sends = []
    for e in range(1, members):
        target = lax.rem(member + e, members)
        copy = pltpu.make_async_remote_copy(
            src_ref=chosen.at[target],
            dst_ref=got.at[e],
            send_sem=send_m.at[e],
            recv_sem=recv_m.at[e],
            device_id=(team, target),
            device_id_type=MESH,
        )
        copy.start()
        sends.append(copy)
    total = chosen[member]
    for e, copy in enumerate(sends):
        copy.wait_recv()
        total = total + got[e + 1]
    own_ref[...] = total
    for copy in copies + sends:
        copy.wait_send()


def update_kernel(cells_ref, rates_ref, base_ref, source_ref, new_ref):
    fields, rows_x, rows_y = base_ref.shape
    cells_x, cells_y = split_cells(cells_ref[...], rows_y)
    count = cells_x.shape[1]
    pick_x = row_mask(cells_x, rows_x)
    pick_y = (lax.broadcasted_iota(jnp.int32, (rows_y, count), 0) == cells_y).astype(F32)
    pick_y = pick_y.astype(BF16)
    pick_y = jnp.concatenate([pick_y, pick_y], axis=1)
    for f in range(fields):
        spread_rates = jnp.where(pick_x, rates_ref[f : f + 1, :], 0.0)
        top = spread_rates.astype(BF16)
        rest = (spread_rates - top.astype(F32)).astype(BF16)
        source = lax.dot_general(
            jnp.concatenate([top, rest], axis=1),
            pick_y,
            (((1,), (1,)), ((), ())),
            preferred_element_type=F32,
        )
        source_ref[f] = source
        new_ref[f] = base_ref[f] + (0.25 * TIME_STEP) * source


def whole(space=VMEM):
    return pl.BlockSpec(memory_space=space)


def shards(
    state_start,
    state_section,
    velocity,
    diffusivity,
    flame_cells,
    block_team,
    w_in,
    w_mid,
    w_low,
    w_out,
):
    teams = lax.axis_size("team")
    members = lax.axis_size("member")
    fields, rows_x, rows_y = state_section.shape
    count = flame_cells.shape[1]
    team_of = block_team.reshape(-1)
    dma = pltpu.SemaphoreType.DMA
    w_in = jnp.swapaxes(w_in, 2, 3)
    hidden = w_in.shape[3]
    blocks, halo_x, halo_y, w_in, w_mid, w_low, w_out = pl.pallas_call(
        functools.partial(share_kernel, teams, members),
        out_shape=(
            jax.ShapeDtypeStruct((members, teams, fields, count), BF16),
            jax.ShapeDtypeStruct((2, fields, rows_y), BF16),
            jax.ShapeDtypeStruct((2, rows_x, rows_y), BF16),
            jax.ShapeDtypeStruct((1, 1, hidden, fields), BF16),
            jax.ShapeDtypeStruct(w_mid.shape, BF16),
            jax.ShapeDtypeStruct(w_low.shape, BF16),
            jax.ShapeDtypeStruct(w_out.shape, BF16),
        ),
        in_specs=[whole(pltpu.HBM)] * 6,
        out_specs=(whole(),) * 7,
        scratch_shapes=[
            VMEM(state_section.shape, F32),
            VMEM(flame_cells.shape, jnp.int32),
            VMEM(w_in.shape, BF16),
            VMEM((2, fields, rows_y), BF16),
            VMEM((2, rows_x, rows_y), BF16),
            dma((6,)),
            dma((teams,)),
            dma((teams,)),
            dma((teams, members)),
            dma((teams, members)),
            dma((4,)),
            dma((4,)),
        ],
        compiler_params=pltpu.CompilerParams(
            collective_id=0, has_side_effects=True, vmem_limit_bytes=GRANT
        ),
        name="share",
    )(state_section, flame_cells, w_in, w_mid, w_low, w_out)
    slots = pl.pallas_call(
        functools.partial(network_kernel, teams, members),
        out_shape=jax.ShapeDtypeStruct((teams * CAP, fields, count), F32),
        in_specs=[whole(pltpu.SMEM)] + [whole()] * 5,
        out_specs=whole(),
        scratch_shapes=[
            VMEM((w_in.shape[2], 2 * count), BF16),
            VMEM((w_mid.shape[2], 2 * count), BF16),
            VMEM((w_low.shape[2], 2 * count), BF16),
            pltpu.SMEM((teams * CAP + 2,), jnp.int32),
            pltpu.SMEM((teams * CAP + 2,), jnp.int32),
        ],
        compiler_params=pltpu.CompilerParams(vmem_limit_bytes=GRANT),
        name="networks",
    )(team_of, blocks.reshape(members * teams, fields, count), w_in, w_mid, w_low, w_out)
    rates, base = pl.pallas_call(
        functools.partial(return_kernel, teams, members),
        out_shape=(
            jax.ShapeDtypeStruct((fields, count), F32),
            jax.ShapeDtypeStruct(state_section.shape, F32),
        ),
        in_specs=[whole(pltpu.SMEM)] * 2 + [whole()] * 6,
        out_specs=(whole(), whole()),
        scratch_shapes=[
            VMEM((teams * CAP, fields, count), F32),
            VMEM((members, fields, count), F32),
            VMEM((members, fields, count), F32),
            dma((teams,)),
            dma((teams,)),
            dma((members,)),
            dma((members,)),
        ],
        compiler_params=pltpu.CompilerParams(
            collective_id=1, has_side_effects=True, vmem_limit_bytes=GRANT
        ),
        name="giveback",
    )(team_of, diffusivity, slots, state_start, state_section, velocity, halo_x, halo_y)
    step = 8 if fields % 8 == 0 else fields
    tile = pl.BlockSpec((step, rows_x, rows_y), lambda i: (i, 0, 0))
    return pl.pallas_call(
        update_kernel,
        grid=(fields // step,),
        out_shape=(
            jax.ShapeDtypeStruct(state_section.shape, F32),
            jax.ShapeDtypeStruct(state_section.shape, F32),
        ),
        in_specs=[
            pl.BlockSpec(flame_cells.shape, lambda i: (0, 0)),
            pl.BlockSpec((step, count), lambda i: (i, 0)),
            tile,
        ],
        out_specs=(tile, tile),
        compiler_params=pltpu.CompilerParams(vmem_limit_bytes=GRANT),
        name="update",
    )(flame_cells, rates, base)


def solution(mesh):
    grid = P(None, "team", "member")
    weights = P("team", "member", None, None)
    placed = (
        grid,
        grid,
        grid,
        P(),
        P(("team", "member"), None),
        P(),
        weights,
        weights,
        weights,
        weights,
    )
    return jax.shard_map(
        shards, mesh=mesh, in_specs=placed, out_specs=(grid, grid), check_vma=False
    )
```

```python
import functools

import jax
import jax.numpy as jnp
from jax import lax
from jax.experimental import pallas as pl
from jax.experimental.pallas import tpu as pltpu
from jax.sharding import PartitionSpec as P

CAP = 2
TIME_STEP = 0.25
GRANT = 16 << 20
MESH = pl.DeviceIdType.MESH
VMEM = pltpu.VMEM
F32 = jnp.float32
BF16 = jnp.bfloat16


def partner(index, flips):
    target = index
    bit = 1
    while bit <= flips:
        if flips & bit:
            target = target + bit - 2 * bit * lax.rem(index // bit, 2)
        bit *= 2
    return target


def split_cells(cells, rows_y):
    shift = rows_y.bit_length() - 1
    assert rows_y == 1 << shift
    return cells >> shift, cells & (rows_y - 1)


def row_mask(cells_x, rows_x):
    count = cells_x.shape[1]
    return lax.broadcasted_iota(jnp.int32, (rows_x, count), 0) == cells_x


def silu(x):
    half = 0.5 * x
    return half + half * jnp.tanh(half)


def greet(team, member, teams, members):
    barrier = pltpu.get_barrier_semaphore()
    for d in range(1, teams):
        pl.semaphore_signal(
            barrier, inc=1, device_id=(partner(team, d), member), device_id_type=MESH
        )
    for e in range(1, members):
        pl.semaphore_signal(
            barrier, inc=1, device_id=(team, partner(member, e)), device_id_type=MESH
        )
    return barrier


def share_kernel(
    teams,
    members,
    section_hbm,
    cells_hbm,
    w_in_hbm,
    w_mid_hbm,
    w_low_hbm,
    w_out_hbm,
    blocks_ref,
    halo_x_ref,
    halo_y_ref,
    w_in_ref,
    w_mid_ref,
    w_low_ref,
    w_out_ref,
    section_ref,
    cells_ref,
    w_in_raw,
    edge_x,
    edge_y,
    load_sem,
    send_t,
    recv_t,
    send_m,
    recv_m,
    send_h,
    recv_h,
):
    team = lax.axis_index("team")
    member = lax.axis_index("member")
    barrier = greet(team, member, teams, members)
    loads = []
    for k, (source, target) in enumerate(
        (
            (section_hbm, section_ref),
            (cells_hbm, cells_ref),
            (w_in_hbm, w_in_raw),
            (w_mid_hbm, w_mid_ref),
            (w_low_hbm, w_low_ref),
            (w_out_hbm, w_out_ref),
        )
    ):
        copy = pltpu.make_async_copy(source, target, load_sem.at[k])
        copy.start()
        loads.append(copy)
    loads[1].wait()
    fields, rows_x, rows_y = section_ref.shape
    cells_x, cells_y = split_cells(cells_ref[...], rows_y)
    count = cells_x.shape[1]
    pick_y = (lax.broadcasted_iota(jnp.int32, (rows_y, count), 0) == cells_y).astype(F32)
    pick_x = row_mask(cells_x, rows_x)
    loads[0].wait()
    flat = section_ref[...].reshape(fields * rows_x, rows_y).astype(BF16)
    taken = jnp.dot(flat, pick_y.astype(BF16), preferred_element_type=F32)
    taken = taken.reshape(fields, rows_x, count)
    own = jnp.sum(jnp.where(pick_x[None], taken, 0.0), axis=1)
    blocks_ref[member, team] = own.astype(BF16)
    pl.semaphore_wait(barrier, teams + members - 2)

    started = []
    t_copies = {}
    for d in range(teams - 1, 0, -1):
        copy = pltpu.make_async_remote_copy(
            src_ref=blocks_ref.at[member, team],
            dst_ref=blocks_ref.at[member, team],
            send_sem=send_t.at[d],
            recv_sem=recv_t.at[d],
            device_id=(partner(team, d), member),
            device_id_type=MESH,
        )
        copy.start()
        t_copies[d] = copy

    def forward(d):
        source = partner(team, d)
        for e in range(members - 1, 0, -1):
            copy = pltpu.make_async_remote_copy(
                src_ref=blocks_ref.at[member, source],
                dst_ref=blocks_ref.at[member, source],
                send_sem=send_m.at[d, e],
                recv_sem=recv_m.at[d, e],
                device_id=(team, partner(member, e)),
                device_id_type=MESH,
            )
            copy.start()
            started.append(copy)

    forward(0)
    edge_x[0] = section_ref[:, rows_x - 1, :].astype(BF16)
    edge_x[1] = section_ref[:, 0, :].astype(BF16)
    lanes = lax.broadcasted_iota(jnp.int32, (rows_x, rows_y), 1)
    low = jnp.zeros((rows_x, rows_y), F32)
    high = jnp.zeros((rows_x, rows_y), F32)
    for f in range(fields):
        plane = section_ref[f]
        here = lanes == f
        high = jnp.where(here, pltpu.roll(plane, (f + 1) % rows_y, 1), high)
        low = jnp.where(here, pltpu.roll(plane, f, 1) if f else plane, low)
    edge_y[0] = high.astype(BF16)
    edge_y[1] = low.astype(BF16)
    halos = []
    for k, (step, edge, halo, along) in enumerate(
        (
            (1, edge_x.at[0], halo_x_ref.at[0], "team"),
            (-1, edge_x.at[1], halo_x_ref.at[1], "team"),
            (1, edge_y.at[0], halo_y_ref.at[0], "member"),
            (-1, edge_y.at[1], halo_y_ref.at[1], "member"),
        )
    ):
        if along == "team":
            device = (lax.rem(team + step + teams, teams), member)
        else:
            device = (team, lax.rem(member + step + members, members))
        copy = pltpu.make_async_remote_copy(
            src_ref=edge,
            dst_ref=halo,
            send_sem=send_h.at[k],
            recv_sem=recv_h.at[k],
            device_id=device,
            device_id_type=MESH,
        )
        copy.start()
        halos.append(copy)
    loads[2].wait()
    w_in_ref[0, 0] = w_in_raw[0, 0].T
    for d in range(1, teams):
        t_copies[d].wait_recv()
        forward(d)
    for copy in started + halos + loads[3:]:
        copy.wait()
    for d in range(1, teams):
        t_copies[d].wait_send()


def network_kernel(
    teams,
    members,
    team_of,
    blocks_ref,
    w_in,
    w_mid,
    w_low,
    w_out,
    slots_ref,
    hidden_one,
    hidden_two,
    hidden_three,
    pick,
    place,
):
    team = lax.axis_index("team")
    fields, count = slots_ref.shape[1:]
    slots_ref[...] = jnp.zeros_like(slots_ref)

    def scan_team(p, found):
        seen = jnp.int32(0)
        for q in range(members):
            mine = (team_of[p * members + q] == team).astype(jnp.int32)
            pick[found] = q * teams + p
            place[found] = p * CAP + seen
            found = found + mine
            seen = seen + mine
        return found

    found = lax.fori_loop(0, teams, scan_team, jnp.int32(0))
    last = jnp.maximum(found - 1, 0)
    pick[found] = pick[last]
    place[found] = place[last]

    def layer(weight, source, target, rows):
        total = weight.shape[2]
        start = 0
        while start < total:
            size = min(rows, total - start)
            span = pl.ds(start, size)
            out = jnp.dot(weight[0, 0, span, :], source, preferred_element_type=F32)
            target[span, :] = silu(out).astype(BF16)
            start += size

    def chunk(i, carry):
        first, second = 2 * i, 2 * i + 1
        states = jnp.concatenate([blocks_ref[pick[first]], blocks_ref[pick[second]]], axis=1)
        layer(w_in, states, hidden_one, 320)
        layer(w_mid, hidden_one[...], hidden_two, 160)
        layer(w_low, hidden_two[...], hidden_three, 80)
        rates = jnp.dot(w_out[0, 0], hidden_three[...], preferred_element_type=F32)
        slots_ref[place[first]] = rates[:, :count]
        slots_ref[place[second]] = rates[:, count:]
        return carry

    lax.fori_loop(0, (found + 1) // 2, chunk, 0)


def flow_base(
    start_ref, section_ref, velocity_ref, spread_ref, halo_x_ref, halo_y_ref, base_ref
):
    fields, rows_x, rows_y = section_ref.shape
    lanes = lax.broadcasted_iota(jnp.int32, (rows_x, rows_y), 1)
    subs = lax.broadcasted_iota(jnp.int32, (rows_x, rows_y), 0)
    half_u = 0.5 * velocity_ref[0]
    half_v = 0.5 * velocity_ref[1]
    low_x = halo_x_ref[0].astype(F32)
    high_x = halo_x_ref[1].astype(F32)
    low_y = halo_y_ref[0].astype(F32)
    high_y = halo_y_ref[1].astype(F32)
    for f in range(fields):
        here = section_ref[f]
        plus_x = jnp.where(
            subs == rows_x - 1, high_x[f : f + 1], pltpu.roll(here, rows_x - 1, 0)
        )
        minus_x = jnp.where(subs == 0, low_x[f : f + 1], pltpu.roll(here, 1, 0))
        plus_y = jnp.where(
            lanes == rows_y - 1,
            pltpu.roll(high_y, rows_y - 1 - f, 1),
            pltpu.roll(here, rows_y - 1, 1),
        )
        edge = pltpu.roll(low_y, (rows_y - f) % rows_y, 1) if f else low_y
        minus_y = jnp.where(lanes == 0, edge, pltpu.roll(here, 1, 1))
        flow = (
            spread_ref[f] * (plus_x + minus_x + plus_y + minus_y - 4.0 * here)
            - half_u * (plus_x - minus_x)
            - half_v * (plus_y - minus_y)
        )
        base_ref[f] = 0.75 * start_ref[f] + 0.25 * (here + TIME_STEP * flow)


def return_kernel(
    teams,
    members,
    team_of,
    spread_ref,
    slots_ref,
    start_ref,
    section_ref,
    velocity_ref,
    halo_x_ref,
    halo_y_ref,
    own_ref,
    base_ref,
    back,
    chosen,
    got,
    send_t,
    recv_t,
    send_m,
    recv_m,
):
    team = lax.axis_index("team")
    member = lax.axis_index("member")
    barrier = greet(team, member, teams, members)
    pl.semaphore_wait(barrier, teams + members - 2)
    copies = []
    for d in range(teams - 1, 0, -1):
        target = partner(team, d)
        copy = pltpu.make_async_remote_copy(
            src_ref=slots_ref.at[pl.ds(target * CAP, CAP)],
            dst_ref=back.at[pl.ds(team * CAP, CAP)],
            send_sem=send_t.at[d],
            recv_sem=recv_t.at[d],
            device_id=(target, member),
            device_id_type=MESH,
        )
        copy.start()
        copies.append(copy)
    back[pl.ds(team * CAP, CAP)] = slots_ref[pl.ds(team * CAP, CAP)]
    assigned = [team_of[team * members + q] for q in range(members)]
    where = []
    for q in range(members):
        rank = jnp.int32(0)
        for other in range(q):
            rank = rank + (assigned[other] == assigned[q]).astype(jnp.int32)
        where.append(assigned[q] * CAP + rank)
    flow_base(
        start_ref, section_ref, velocity_ref, spread_ref, halo_x_ref, halo_y_ref, base_ref
    )
    for copy in copies:
        copy.wait_recv()
    for q in range(members):
        chosen[q] = back[where[q]]
    sends = []
    for e in range(members - 1, 0, -1):
        target = partner(member, e)
        copy = pltpu.make_async_remote_copy(
            src_ref=chosen.at[target],
            dst_ref=got.at[e],
            send_sem=send_m.at[e],
            recv_sem=recv_m.at[e],
            device_id=(team, target),
            device_id_type=MESH,
        )
        copy.start()
        sends.append(copy)
    total = chosen[member]
    for e in range(1, members):
        sends[members - 1 - e].wait_recv()
        total = total + got[e]
    own_ref[...] = total
    for copy in copies + sends:
        copy.wait_send()


def update_kernel(cells_ref, rates_ref, base_ref, source_ref, new_ref):
    fields, rows_x, rows_y = base_ref.shape
    cells_x, cells_y = split_cells(cells_ref[...], rows_y)
    count = cells_x.shape[1]
    pick_x = row_mask(cells_x, rows_x)
    pick_y = (lax.broadcasted_iota(jnp.int32, (rows_y, count), 0) == cells_y).astype(F32)
    pick_y = pick_y.astype(BF16)
    pick_y = jnp.concatenate([pick_y, pick_y], axis=1)
    for f in range(fields):
        spread_rates = jnp.where(pick_x, rates_ref[f : f + 1, :], 0.0)
        top = spread_rates.astype(BF16)
        rest = (spread_rates - top.astype(F32)).astype(BF16)
        source = lax.dot_general(
            jnp.concatenate([top, rest], axis=1),
            pick_y,
            (((1,), (1,)), ((), ())),
            preferred_element_type=F32,
        )
        source_ref[f] = source
        new_ref[f] = base_ref[f] + (0.25 * TIME_STEP) * source


def whole(space=VMEM):
    return pl.BlockSpec(memory_space=space)


def shards(
    state_start,
    state_section,
    velocity,
    diffusivity,
    flame_cells,
    block_team,
    w_in,
    w_mid,
    w_low,
    w_out,
):
    teams = lax.axis_size("team")
    members = lax.axis_size("member")
    fields, rows_x, rows_y = state_section.shape
    count = flame_cells.shape[1]
    team_of = block_team.reshape(-1)
    dma = pltpu.SemaphoreType.DMA
    w_in = jnp.swapaxes(w_in, 2, 3)
    hidden = w_in.shape[3]
    blocks, halo_x, halo_y, w_in, w_mid, w_low, w_out = pl.pallas_call(
        functools.partial(share_kernel, teams, members),
        out_shape=(
            jax.ShapeDtypeStruct((members, teams, fields, count), BF16),
            jax.ShapeDtypeStruct((2, fields, rows_y), BF16),
            jax.ShapeDtypeStruct((2, rows_x, rows_y), BF16),
            jax.ShapeDtypeStruct((1, 1, hidden, fields), BF16),
            jax.ShapeDtypeStruct(w_mid.shape, BF16),
            jax.ShapeDtypeStruct(w_low.shape, BF16),
            jax.ShapeDtypeStruct(w_out.shape, BF16),
        ),
        in_specs=[whole(pltpu.HBM)] * 6,
        out_specs=(whole(),) * 7,
        scratch_shapes=[
            VMEM(state_section.shape, F32),
            VMEM(flame_cells.shape, jnp.int32),
            VMEM(w_in.shape, BF16),
            VMEM((2, fields, rows_y), BF16),
            VMEM((2, rows_x, rows_y), BF16),
            dma((6,)),
            dma((teams,)),
            dma((teams,)),
            dma((teams, members)),
            dma((teams, members)),
            dma((4,)),
            dma((4,)),
        ],
        compiler_params=pltpu.CompilerParams(
            collective_id=0, has_side_effects=True, vmem_limit_bytes=GRANT
        ),
        name="share",
    )(*[pltpu.with_memory_space_constraint(x, pltpu.HBM)
       for x in (state_section, flame_cells, w_in, w_mid, w_low, w_out)])
    slots = pl.pallas_call(
        functools.partial(network_kernel, teams, members),
        out_shape=jax.ShapeDtypeStruct((teams * CAP, fields, count), F32),
        in_specs=[whole(pltpu.SMEM)] + [whole()] * 5,
        out_specs=whole(),
        scratch_shapes=[
            VMEM((w_in.shape[2], 2 * count), BF16),
            VMEM((w_mid.shape[2], 2 * count), BF16),
            VMEM((w_low.shape[2], 2 * count), BF16),
            pltpu.SMEM((teams * CAP + 2,), jnp.int32),
            pltpu.SMEM((teams * CAP + 2,), jnp.int32),
        ],
        compiler_params=pltpu.CompilerParams(vmem_limit_bytes=GRANT),
        name="networks",
    )(team_of, blocks.reshape(members * teams, fields, count), w_in, w_mid, w_low, w_out)
    rates, base = pl.pallas_call(
        functools.partial(return_kernel, teams, members),
        out_shape=(
            jax.ShapeDtypeStruct((fields, count), F32),
            jax.ShapeDtypeStruct(state_section.shape, F32),
        ),
        in_specs=[whole(pltpu.SMEM)] * 2 + [whole()] * 6,
        out_specs=(whole(), whole()),
        scratch_shapes=[
            VMEM((teams * CAP, fields, count), F32),
            VMEM((members, fields, count), F32),
            VMEM((members, fields, count), F32),
            dma((teams,)),
            dma((teams,)),
            dma((members,)),
            dma((members,)),
        ],
        compiler_params=pltpu.CompilerParams(
            collective_id=1, has_side_effects=True, vmem_limit_bytes=GRANT
        ),
        name="giveback",
    )(team_of, diffusivity, slots, state_start, state_section, velocity, halo_x, halo_y)
    step = 8 if fields % 8 == 0 else fields
    tile = pl.BlockSpec((step, rows_x, rows_y), lambda i: (i, 0, 0))
    return pl.pallas_call(
        update_kernel,
        grid=(fields // step,),
        out_shape=(
            jax.ShapeDtypeStruct(state_section.shape, F32),
            jax.ShapeDtypeStruct(state_section.shape, F32),
        ),
        in_specs=[
            pl.BlockSpec(flame_cells.shape, lambda i: (0, 0)),
            pl.BlockSpec((step, count), lambda i: (i, 0)),
            tile,
        ],
        out_specs=(tile, tile),
        compiler_params=pltpu.CompilerParams(vmem_limit_bytes=GRANT),
        name="update",
    )(flame_cells, rates, base)


def solution(mesh):
    grid = P(None, "team", "member")
    weights = P("team", "member", None, None)
    placed = (
        grid,
        grid,
        grid,
        P(),
        P(("team", "member"), None),
        P(),
        weights,
        weights,
        weights,
        weights,
    )
    return jax.shard_map(
        shards, mesh=mesh, in_specs=placed, out_specs=(grid, grid), check_vma=False
    )
```

```python
import functools

import jax
import jax.numpy as jnp
from jax import lax
from jax.experimental import pallas as pl
from jax.experimental.pallas import tpu as pltpu
from jax.sharding import PartitionSpec as P

CAP = 2
TIME_STEP = 0.25
GRANT = 16 << 20
MESH = pl.DeviceIdType.MESH
VMEM = pltpu.VMEM
F32 = jnp.float32
BF16 = jnp.bfloat16


def partner(index, flips):
    target = index
    bit = 1
    while bit <= flips:
        if flips & bit:
            target = target + bit - 2 * bit * lax.rem(index // bit, 2)
        bit *= 2
    return target


def split_cells(cells, rows_y):
    shift = rows_y.bit_length() - 1
    assert rows_y == 1 << shift
    return cells >> shift, cells & (rows_y - 1)


def row_mask(cells_x, rows_x):
    count = cells_x.shape[1]
    return lax.broadcasted_iota(jnp.int32, (rows_x, count), 0) == cells_x


def silu(x):
    half = 0.5 * x
    return half + half * jnp.tanh(half)


def greet(team, member, teams, members):
    barrier = pltpu.get_barrier_semaphore()
    for d in range(1, teams):
        pl.semaphore_signal(
            barrier, inc=1, device_id=(partner(team, d), member), device_id_type=MESH
        )
    for e in range(1, members):
        pl.semaphore_signal(
            barrier, inc=1, device_id=(team, partner(member, e)), device_id_type=MESH
        )
    return barrier


def share_kernel(
    teams,
    members,
    section_hbm,
    cells_hbm,
    w_in_hbm,
    w_mid_hbm,
    w_low_hbm,
    w_out_hbm,
    blocks_ref,
    halo_x_ref,
    halo_y_ref,
    w_in_ref,
    w_mid_ref,
    w_low_ref,
    w_out_ref,
    section_ref,
    cells_ref,
    w_in_raw,
    edge_x,
    edge_y,
    load_sem,
    send_t,
    recv_t,
    send_m,
    recv_m,
    send_h,
    recv_h,
):
    team = lax.axis_index("team")
    member = lax.axis_index("member")
    barrier = greet(team, member, teams, members)
    loads = []
    for k, (source, target) in enumerate(
        (
            (section_hbm, section_ref),
            (cells_hbm, cells_ref),
            (w_in_hbm, w_in_raw),
            (w_mid_hbm, w_mid_ref),
            (w_low_hbm, w_low_ref),
            (w_out_hbm, w_out_ref),
        )
    ):
        loads.append(pltpu.make_async_copy(source, target, load_sem.at[k]))
    loads[1].start()
    loads[0].start()
    loads[1].wait()
    fields, rows_x, rows_y = section_ref.shape
    cells_x, cells_y = split_cells(cells_ref[...], rows_y)
    count = cells_x.shape[1]
    pick_y = (lax.broadcasted_iota(jnp.int32, (rows_y, count), 0) == cells_y).astype(F32)
    pick_x = row_mask(cells_x, rows_x)
    loads[0].wait()
    for copy in loads[2:]:
        copy.start()
    flat = section_ref[...].reshape(fields * rows_x, rows_y).astype(BF16)
    taken = jnp.dot(flat, pick_y.astype(BF16), preferred_element_type=F32)
    taken = taken.reshape(fields, rows_x, count)
    own = jnp.sum(jnp.where(pick_x[None], taken, 0.0), axis=1)
    blocks_ref[member, team] = own.astype(BF16)
    pl.semaphore_wait(barrier, teams + members - 2)

    started = []
    t_copies = {}
    for d in range(teams - 1, 0, -1):
        copy = pltpu.make_async_remote_copy(
            src_ref=blocks_ref.at[member, team],
            dst_ref=blocks_ref.at[member, team],
            send_sem=send_t.at[d],
            recv_sem=recv_t.at[d],
            device_id=(partner(team, d), member),
            device_id_type=MESH,
        )
        copy.start()
        t_copies[d] = copy

    def forward(d):
        source = partner(team, d)
        for e in range(members - 1, 0, -1):
            copy = pltpu.make_async_remote_copy(
                src_ref=blocks_ref.at[member, source],
                dst_ref=blocks_ref.at[member, source],
                send_sem=send_m.at[d, e],
                recv_sem=recv_m.at[d, e],
                device_id=(team, partner(member, e)),
                device_id_type=MESH,
            )
            copy.start()
            started.append(copy)

    forward(0)
    edge_x[0] = section_ref[:, rows_x - 1, :].astype(BF16)
    edge_x[1] = section_ref[:, 0, :].astype(BF16)
    lanes = lax.broadcasted_iota(jnp.int32, (rows_x, rows_y), 1)
    low = jnp.zeros((rows_x, rows_y), F32)
    high = jnp.zeros((rows_x, rows_y), F32)
    for f in range(fields):
        plane = section_ref[f]
        here = lanes == f
        high = jnp.where(here, pltpu.roll(plane, (f + 1) % rows_y, 1), high)
        low = jnp.where(here, pltpu.roll(plane, f, 1) if f else plane, low)
    edge_y[0] = high.astype(BF16)
    edge_y[1] = low.astype(BF16)
    halos = []
    for k, (step, edge, halo, along) in enumerate(
        (
            (1, edge_x.at[0], halo_x_ref.at[0], "team"),
            (-1, edge_x.at[1], halo_x_ref.at[1], "team"),
            (1, edge_y.at[0], halo_y_ref.at[0], "member"),
            (-1, edge_y.at[1], halo_y_ref.at[1], "member"),
        )
    ):
        if along == "team":
            device = (lax.rem(team + step + teams, teams), member)
        else:
            device = (team, lax.rem(member + step + members, members))
        copy = pltpu.make_async_remote_copy(
            src_ref=edge,
            dst_ref=halo,
            send_sem=send_h.at[k],
            recv_sem=recv_h.at[k],
            device_id=device,
            device_id_type=MESH,
        )
        copy.start()
        halos.append(copy)
    loads[2].wait()
    w_in_ref[0, 0] = w_in_raw[0, 0].T
    for d in range(1, teams):
        t_copies[d].wait_recv()
        forward(d)
    for copy in started + halos + loads[3:]:
        copy.wait()
    for d in range(1, teams):
        t_copies[d].wait_send()


def network_kernel(
    teams,
    members,
    team_of,
    blocks_ref,
    w_in,
    w_mid,
    w_low,
    w_out,
    slots_ref,
    hidden_one,
    hidden_two,
    hidden_three,
    pick,
    place,
):
    team = lax.axis_index("team")
    fields, count = slots_ref.shape[1:]
    slots_ref[...] = jnp.zeros_like(slots_ref)

    def scan_team(p, found):
        seen = jnp.int32(0)
        for q in range(members):
            mine = (team_of[p * members + q] == team).astype(jnp.int32)
            pick[found] = q * teams + p
            place[found] = p * CAP + seen
            found = found + mine
            seen = seen + mine
        return found

    found = lax.fori_loop(0, teams, scan_team, jnp.int32(0))
    last = jnp.maximum(found - 1, 0)
    pick[found] = pick[last]
    place[found] = place[last]

    def layer(weight, source, target, rows):
        total = weight.shape[2]
        start = 0
        while start < total:
            size = min(rows, total - start)
            span = pl.ds(start, size)
            out = jnp.dot(weight[0, 0, span, :], source, preferred_element_type=F32)
            target[span, :] = silu(out).astype(BF16)
            start += size

    def chunk(i, carry):
        first, second = 2 * i, 2 * i + 1
        states = jnp.concatenate([blocks_ref[pick[first]], blocks_ref[pick[second]]], axis=1)
        layer(w_in, states, hidden_one, 320)
        layer(w_mid, hidden_one[...], hidden_two, 160)
        layer(w_low, hidden_two[...], hidden_three, 80)
        rates = jnp.dot(w_out[0, 0], hidden_three[...], preferred_element_type=F32)
        slots_ref[place[first]] = rates[:, :count]
        slots_ref[place[second]] = rates[:, count:]
        return carry

    lax.fori_loop(0, (found + 1) // 2, chunk, 0)


def flow_base(
    start_ref, section_ref, velocity_ref, spread_ref, halo_x_ref, halo_y_ref, base_ref
):
    fields, rows_x, rows_y = section_ref.shape
    lanes = lax.broadcasted_iota(jnp.int32, (rows_x, rows_y), 1)
    subs = lax.broadcasted_iota(jnp.int32, (rows_x, rows_y), 0)
    half_u = 0.5 * velocity_ref[0]
    half_v = 0.5 * velocity_ref[1]
    low_x = halo_x_ref[0].astype(F32)
    high_x = halo_x_ref[1].astype(F32)
    low_y = halo_y_ref[0].astype(F32)
    high_y = halo_y_ref[1].astype(F32)
    for f in range(fields):
        here = section_ref[f]
        plus_x = jnp.where(
            subs == rows_x - 1, high_x[f : f + 1], pltpu.roll(here, rows_x - 1, 0)
        )
        minus_x = jnp.where(subs == 0, low_x[f : f + 1], pltpu.roll(here, 1, 0))
        plus_y = jnp.where(
            lanes == rows_y - 1,
            pltpu.roll(high_y, rows_y - 1 - f, 1),
            pltpu.roll(here, rows_y - 1, 1),
        )
        edge = pltpu.roll(low_y, (rows_y - f) % rows_y, 1) if f else low_y
        minus_y = jnp.where(lanes == 0, edge, pltpu.roll(here, 1, 1))
        flow = (
            spread_ref[f] * (plus_x + minus_x + plus_y + minus_y - 4.0 * here)
            - half_u * (plus_x - minus_x)
            - half_v * (plus_y - minus_y)
        )
        base_ref[f] = 0.75 * start_ref[f] + 0.25 * (here + TIME_STEP * flow)


def return_kernel(
    teams,
    members,
    team_of,
    spread_ref,
    slots_ref,
    start_ref,
    section_ref,
    velocity_ref,
    halo_x_ref,
    halo_y_ref,
    own_ref,
    base_ref,
    back,
    chosen,
    got,
    send_t,
    recv_t,
    send_m,
    recv_m,
):
    team = lax.axis_index("team")
    member = lax.axis_index("member")
    barrier = greet(team, member, teams, members)
    pl.semaphore_wait(barrier, teams + members - 2)
    copies = []
    for d in range(teams - 1, 0, -1):
        target = partner(team, d)
        copy = pltpu.make_async_remote_copy(
            src_ref=slots_ref.at[pl.ds(target * CAP, CAP)],
            dst_ref=back.at[pl.ds(team * CAP, CAP)],
            send_sem=send_t.at[d],
            recv_sem=recv_t.at[d],
            device_id=(target, member),
            device_id_type=MESH,
        )
        copy.start()
        copies.append(copy)
    back[pl.ds(team * CAP, CAP)] = slots_ref[pl.ds(team * CAP, CAP)]
    assigned = [team_of[team * members + q] for q in range(members)]
    where = []
    for q in range(members):
        rank = jnp.int32(0)
        for other in range(q):
            rank = rank + (assigned[other] == assigned[q]).astype(jnp.int32)
        where.append(assigned[q] * CAP + rank)
    flow_base(
        start_ref, section_ref, velocity_ref, spread_ref, halo_x_ref, halo_y_ref, base_ref
    )
    for copy in copies:
        copy.wait_recv()
    for q in range(members):
        chosen[q] = back[where[q]]
    sends = []
    for e in range(members - 1, 0, -1):
        target = partner(member, e)
        copy = pltpu.make_async_remote_copy(
            src_ref=chosen.at[target],
            dst_ref=got.at[e],
            send_sem=send_m.at[e],
            recv_sem=recv_m.at[e],
            device_id=(team, target),
            device_id_type=MESH,
        )
        copy.start()
        sends.append(copy)
    total = chosen[member]
    for e in range(1, members):
        sends[members - 1 - e].wait_recv()
        total = total + got[e]
    own_ref[...] = total
    for copy in copies + sends:
        copy.wait_send()


def update_kernel(
    groups, cells_ref, rates_ref, base_ref, source_out, new_out, source_ref, new_ref, sems
):
    fields, rows_x, rows_y = base_ref.shape
    cells_x, cells_y = split_cells(cells_ref[...], rows_y)
    count = cells_x.shape[1]
    pick_x = row_mask(cells_x, rows_x)
    pick_y = (lax.broadcasted_iota(jnp.int32, (rows_y, count), 0) == cells_y).astype(F32)
    pick_y = pick_y.astype(BF16)
    pick_y = jnp.concatenate([pick_y, pick_y], axis=1)
    group = fields // groups
    copies = []
    for f in range(fields):
        spread_rates = jnp.where(pick_x, rates_ref[f : f + 1, :], 0.0)
        top = spread_rates.astype(BF16)
        rest = (spread_rates - top.astype(F32)).astype(BF16)
        source = lax.dot_general(
            jnp.concatenate([top, rest], axis=1),
            pick_y,
            (((1,), (1,)), ((), ())),
            preferred_element_type=F32,
        )
        source_ref[f] = source
        new_ref[f] = base_ref[f] + (0.25 * TIME_STEP) * source
        if (f + 1) % group == 0:
            span = pl.ds(f + 1 - group, group)
            for k, (held, out) in enumerate(((source_ref, source_out), (new_ref, new_out))):
                copy = pltpu.make_async_copy(held.at[span], out.at[span], sems.at[k, f // group])
                copy.start()
                copies.append(copy)
    for copy in copies:
        copy.wait()


def whole(space=VMEM):
    return pl.BlockSpec(memory_space=space)


def shards(
    state_start,
    state_section,
    velocity,
    diffusivity,
    flame_cells,
    block_team,
    w_in,
    w_mid,
    w_low,
    w_out,
):
    teams = lax.axis_size("team")
    members = lax.axis_size("member")
    fields, rows_x, rows_y = state_section.shape
    count = flame_cells.shape[1]
    team_of = block_team.reshape(-1)
    dma = pltpu.SemaphoreType.DMA
    w_in = jnp.swapaxes(w_in, 2, 3)
    hidden = w_in.shape[3]
    blocks, halo_x, halo_y, w_in, w_mid, w_low, w_out = pl.pallas_call(
        functools.partial(share_kernel, teams, members),
        out_shape=(
            jax.ShapeDtypeStruct((members, teams, fields, count), BF16),
            jax.ShapeDtypeStruct((2, fields, rows_y), BF16),
            jax.ShapeDtypeStruct((2, rows_x, rows_y), BF16),
            jax.ShapeDtypeStruct((1, 1, hidden, fields), BF16),
            jax.ShapeDtypeStruct(w_mid.shape, BF16),
            jax.ShapeDtypeStruct(w_low.shape, BF16),
            jax.ShapeDtypeStruct(w_out.shape, BF16),
        ),
        in_specs=[whole(pltpu.HBM)] * 6,
        out_specs=(whole(),) * 7,
        scratch_shapes=[
            VMEM(state_section.shape, F32),
            VMEM(flame_cells.shape, jnp.int32),
            VMEM(w_in.shape, BF16),
            VMEM((2, fields, rows_y), BF16),
            VMEM((2, rows_x, rows_y), BF16),
            dma((6,)),
            dma((teams,)),
            dma((teams,)),
            dma((teams, members)),
            dma((teams, members)),
            dma((4,)),
            dma((4,)),
        ],
        compiler_params=pltpu.CompilerParams(
            collective_id=0, has_side_effects=True, vmem_limit_bytes=GRANT
        ),
        name="share",
    )(*[pltpu.with_memory_space_constraint(x, pltpu.HBM)
       for x in (state_section, flame_cells, w_in, w_mid, w_low, w_out)])
    slots = pl.pallas_call(
        functools.partial(network_kernel, teams, members),
        out_shape=jax.ShapeDtypeStruct((teams * CAP, fields, count), F32),
        in_specs=[whole(pltpu.SMEM)] + [whole()] * 5,
        out_specs=whole(),
        scratch_shapes=[
            VMEM((w_in.shape[2], 2 * count), BF16),
            VMEM((w_mid.shape[2], 2 * count), BF16),
            VMEM((w_low.shape[2], 2 * count), BF16),
            pltpu.SMEM((teams * CAP + 2,), jnp.int32),
            pltpu.SMEM((teams * CAP + 2,), jnp.int32),
        ],
        compiler_params=pltpu.CompilerParams(vmem_limit_bytes=GRANT),
        name="networks",
    )(team_of, blocks.reshape(members * teams, fields, count), w_in, w_mid, w_low, w_out)
    rates, base = pl.pallas_call(
        functools.partial(return_kernel, teams, members),
        out_shape=(
            jax.ShapeDtypeStruct((fields, count), F32),
            jax.ShapeDtypeStruct(state_section.shape, F32),
        ),
        in_specs=[whole(pltpu.SMEM)] * 2 + [whole()] * 6,
        out_specs=(whole(), whole()),
        scratch_shapes=[
            VMEM((teams * CAP, fields, count), F32),
            VMEM((members, fields, count), F32),
            VMEM((members, fields, count), F32),
            dma((teams,)),
            dma((teams,)),
            dma((members,)),
            dma((members,)),
        ],
        compiler_params=pltpu.CompilerParams(
            collective_id=1, has_side_effects=True, vmem_limit_bytes=GRANT
        ),
        name="giveback",
    )(team_of, diffusivity, slots, state_start, state_section, velocity, halo_x, halo_y)
    groups = 6 if fields % 6 == 0 else fields
    return pl.pallas_call(
        functools.partial(update_kernel, groups),
        out_shape=(
            jax.ShapeDtypeStruct(state_section.shape, F32),
            jax.ShapeDtypeStruct(state_section.shape, F32),
        ),
        in_specs=[whole()] * 3,
        out_specs=(whole(pl.ANY), whole(pl.ANY)),
        scratch_shapes=[
            VMEM(state_section.shape, F32),
            VMEM(state_section.shape, F32),
            dma((2, groups)),
        ],
        compiler_params=pltpu.CompilerParams(vmem_limit_bytes=GRANT),
        name="update",
    )(flame_cells, rates, base)


def solution(mesh):
    grid = P(None, "team", "member")
    weights = P("team", "member", None, None)
    placed = (
        grid,
        grid,
        grid,
        P(),
        P(("team", "member"), None),
        P(),
        weights,
        weights,
        weights,
        weights,
    )
    return jax.shard_map(
        shards, mesh=mesh, in_specs=placed, out_specs=(grid, grid), check_vma=False
    )
```
